256 devices in a mesh: dp: 8 (over y, core), expert: 32 (over z, x).
Axes of the slice: x: 4, y: 4, z: 8, core: 2. Of those that a mesh axis runs over, the one named last changes fastest.
Arguments:
- tokens: bfloat16 [32768, 2048], P(('dp', 'expert')), may hold values from -6 to 6
- expert_ids: int32 [32768, 8], P(('dp', 'expert')), may hold values from 0 to 31, all different within a row
- gate_vals: float32 [32768, 8], P(('dp', 'expert')), may hold values from 0.05 to 0.5
- replica_plan: int32 [32], replicated, may hold values from 0 to 1, as said below
- expert_weights: bfloat16 [32, 3, 2048, 768], P('expert'), may hold values from -0.125 to 0.125
- cotangent: bfloat16 [32768, 2048], P(('dp', 'expert')), may hold values from -6 to 6
Outputs:
- output: bfloat16 [32768, 2048], P(('dp', 'expert'))
- gate_grads: float32 [32768, 8], P(('dp', 'expert'))
- input_grad: bfloat16 [32768, 2048], P(('dp', 'expert'))
- weight_grads: bfloat16 [32, 3, 2048, 768], P('expert', None, 'dp')
The draws below stay inside these ranges and needn't reach their ends.
Inputs may be any that keep to these rules, and one draw needn't show every extreme that they name: `replica_plan`: of experts x and x + 16 exactly one is marked.
All inputs are finite; a program needn't handle non-finite values.
Results may differ from the reference program's by a relative error of at most 0.017.
Values may be sent and summed in bfloat16 or wider, within the bound.
A program may use at most 128 MiB of HBM per device.

```python
import math
import jax
import jax.numpy as jnp
from jax import lax

D = 2048
FF = 768
TOPK = 8
TOK_DEV = 128
EXPERTS = 32
CAP = 10
TOKENS = 32768
N_DP = 8
N_EXPERT = 32


def draw_replica_plan(key, part):
    half = EXPERTS // 2
    pick = jax.random.randint(key, (half,), 0, 2).astype(jnp.int32)
    labels = jnp.arange(EXPERTS, dtype=jnp.int32)
    upper = (labels >= half).astype(jnp.int32)
    return (pick[labels % half] == upper).astype(jnp.int32)


def block_levels(stream_key, extent, pieces, low, largest):
    gain, own = 1.0, jax.random.fold_in(stream_key, 6)
    for dim, shards_of in pieces:
        steps = jnp.exp(jax.random.uniform(jax.random.fold_in(own, dim), (shards_of,), jnp.float32, low / len(pieces), largest / len(pieces)))
        gain = gain * jnp.repeat(steps, extent[dim] // shards_of).reshape([-1 if axis == dim else 1 for axis in range(len(extent))])
    return gain


def picks_of(own_key, rows, amount, top, lift):
    ranking = jax.random.permutation(jax.random.fold_in(own_key, 1), amount)
    boost = ranking
    for power in range(3):
        boost = boost * boost // amount
    boost = boost * lift // amount
    chance = jax.random.randint(jax.random.fold_in(own_key, 2), (rows, amount), 0, 4096) + boost
    holders = jax.random.permutation(jax.random.fold_in(own_key, 3), rows)[jnp.arange(amount) % rows]
    chance = jnp.where(jnp.arange(rows)[:, None] == holders[None, :], 1 << 14, chance)
    score = chance * amount + jnp.arange(amount)
    return lax.top_k(score.astype(jnp.int32), top)[1].astype(jnp.int32)


def centred(own_key, dims, deviation, reach, pieces=(), kind=jnp.bfloat16):
    factor_of = block_levels(own_key, dims, pieces, -0.22, 0.18) if pieces else 1.0
    array = jax.random.normal(own_key, dims, jnp.float32) * deviation * factor_of
    return jnp.minimum(jnp.maximum(array, -reach), reach).astype(kind)


def setup_inputs(seed: int = 0) -> dict:
    arg_keys = jax.random.split(jax.random.key(seed), 7)
    return {
        "tokens": centred(arg_keys[0], (TOKENS, D), 1.0, 6.0, ((0, 256),)),
        "expert_ids": picks_of(arg_keys[1], TOKENS, EXPERTS, TOPK, 4096),
        "gate_vals": jnp.clip(jnp.exp(math.log(0.5) - 2.3025851 * jax.random.uniform(arg_keys[2], (TOKENS, TOPK), jnp.float32) ** block_levels(arg_keys[2], (TOKENS, TOPK), ((0, 256),), -0.2, 0.2)), 0.05, 0.5),
        "replica_plan": draw_replica_plan(jax.random.fold_in(arg_keys[6], 71), 0),
        "expert_weights": centred(arg_keys[4], (EXPERTS, 3, D, FF), D ** -0.5, 0.125, ((0, 32),)),
        "cotangent": centred(arg_keys[5], (TOKENS, D), 1.0, 6.0, ((0, 256),)),
    }


def expert_pass(args):
    xb, db, w = args
    gate_part = jnp.dot(xb, w[0], preferred_element_type=jnp.float32)
    up_part = jnp.dot(xb, w[1], preferred_element_type=jnp.float32)
    sigma = jax.nn.sigmoid(gate_part)
    active = gate_part * sigma
    hidden = (active * up_part).astype(jnp.bfloat16)
    result = lax.dot_general(hidden, w[2], (((1,), (1,)), ((), ())), preferred_element_type=jnp.float32).astype(jnp.bfloat16)
    hgrad = jnp.dot(db, w[2], preferred_element_type=jnp.float32)
    d_gate = (hgrad * up_part * sigma * (1.0 + gate_part * (1.0 - sigma))).astype(jnp.bfloat16)
    d_up = (hgrad * active).astype(jnp.bfloat16)
    row_grad = (lax.dot_general(d_gate, w[0], (((1,), (1,)), ((), ())), preferred_element_type=jnp.float32)
                + lax.dot_general(d_up, w[1], (((1,), (1,)), ((), ())), preferred_element_type=jnp.float32)).astype(jnp.bfloat16)
    grad_gate = jnp.dot(xb.T, d_gate, preferred_element_type=jnp.float32).astype(jnp.bfloat16)
    grad_up = jnp.dot(xb.T, d_up, preferred_element_type=jnp.float32).astype(jnp.bfloat16)
    grad_down = jnp.dot(db.T, hidden, preferred_element_type=jnp.float32).astype(jnp.bfloat16)
    return result, row_grad, jnp.stack([grad_gate, grad_up, grad_down])


def reference(tokens, expert_ids, gate_vals, replica_plan, expert_weights, cotangent):
    slots = 2 * CAP
    rows = TOK_DEV * TOPK
    total = EXPERTS * N_EXPERT * slots
    ids = expert_ids.reshape(N_DP, N_EXPERT, rows)
    labels = jnp.arange(EXPERTS, dtype=jnp.int32)
    onehot = (ids[..., None] == labels).astype(jnp.int32)
    rank = jnp.sum((jnp.cumsum(onehot, axis=2) - onehot) * onehot, axis=3)
    marked = jnp.sum(onehot * replica_plan[None, None, None, :], axis=3)
    keep = (rank < CAP) | ((marked == 1) & (rank < slots))
    source = jnp.arange(N_EXPERT, dtype=jnp.int32)[None, :, None]
    dest = jnp.where(keep, ids * (N_EXPERT * slots) + source * slots + rank, total).astype(jnp.int32)
    gates = gate_vals.reshape(N_DP, N_EXPERT, rows)
    toks = tokens.reshape(N_DP, N_EXPERT, TOK_DEV, D)
    dys = cotangent.reshape(N_DP, N_EXPERT, TOK_DEV, D)

    def per_row(carry, inputs):
        tok_d, dy_d, dest_d, gate_d = inputs
        flat_dest = dest_d.reshape(-1)
        xr = jnp.repeat(tok_d, TOPK, axis=1).reshape(-1, D)
        dyr32 = jnp.repeat(dy_d, TOPK, axis=1).reshape(-1, D).astype(jnp.float32)
        dyr = (gate_d.reshape(-1)[:, None] * dyr32).astype(jnp.bfloat16)
        xbuf = jnp.zeros((total, D), jnp.bfloat16).at[flat_dest].set(xr, mode="drop")
        dybuf = jnp.zeros((total, D), jnp.bfloat16).at[flat_dest].set(dyr, mode="drop")
        outs, rgrads, grads = lax.map(expert_pass, (xbuf.reshape(EXPERTS, N_EXPERT * slots, D),
                                                    dybuf.reshape(EXPERTS, N_EXPERT * slots, D), expert_weights))
        outs = outs.reshape(total, D)
        rgrads = rgrads.reshape(total, D)
        valid = (flat_dest < total)[:, None]
        index = jnp.minimum(flat_dest, total - 1)
        pair_out = jnp.where(valid, outs[index].astype(jnp.float32), 0.0)
        pair_grad = jnp.where(valid, rgrads[index].astype(jnp.float32), 0.0)
        weighted = gate_d.reshape(-1)[:, None] * pair_out
        out_d = jnp.sum(weighted.reshape(N_EXPERT, TOK_DEV, TOPK, D), axis=2).astype(jnp.bfloat16)
        gg_d = jnp.sum(dyr32 * pair_out, axis=1).reshape(N_EXPERT, TOK_DEV, TOPK)
        dx_d = jnp.sum(pair_grad.reshape(N_EXPERT, TOK_DEV, TOPK, D), axis=2).astype(jnp.bfloat16)
        return carry + grads.astype(jnp.float32), (out_d, gg_d, dx_d)

    start = jnp.zeros((EXPERTS, 3, D, FF), jnp.float32)
    weight_sum, (out_all, gg_all, dx_all) = lax.scan(per_row, start, (toks, dys, dest, gates))
    output = out_all.reshape(TOKENS, D)
    gate_grads = gg_all.reshape(TOKENS, TOPK)
    input_grad = dx_all.reshape(TOKENS, D)
    weight_grads = weight_sum.astype(jnp.bfloat16)
    return (output, gate_grads, input_grad, weight_grads)
```

```python
import functools

import jax
import jax.numpy as jnp
from jax import lax
from jax.experimental import pallas as pl
from jax.experimental.pallas import tpu as pltpu
from jax.sharding import PartitionSpec as P

COLS = 4
RING = 8
HOPS = 3
FAR = 6
PAIRS = 4
LANES = 128
BF16, F32 = jnp.bfloat16, jnp.float32


def place():
    here = lax.axis_index("expert")
    z, x = here // COLS, here % COLS
    up = ((z + 1) % RING) * COLS + x
    down = ((z + RING - 1) % RING) * COLS + x
    right = [z * COLS + (x + d) % COLS for d in range(COLS)]
    left = [z * COLS + (x + COLS - d) % COLS for d in range(COLS)]
    return z, x, up, down, right, left


def copy_to(src, dst, send_sem, recv_sem, device):
    return pltpu.make_async_remote_copy(
        src_ref=src,
        dst_ref=dst,
        send_sem=send_sem,
        recv_sem=recv_sem,
        device_id={"expert": device},
        device_id_type=pl.DeviceIdType.MESH,
    )


def meet(up, down, right):
    barrier = pltpu.get_barrier_semaphore()
    peers = [up, down] + right[1:]
    for peer in peers:
        pl.semaphore_signal(
            barrier, inc=1, device_id={"expert": peer}, device_id_type=pl.DeviceIdType.MESH
        )
    pl.semaphore_wait(barrier, len(peers))


def dispatch_kernel(
    cap, plan, tok, cot, info, tok_rows, cot_rows, spread,
    tok_ring, cot_ring, info_ring, tok_sel, cot_sel,
    ring_send, ring_recv, row_send, row_recv, own_sem,
):
    z, x, up, down, right, _ = place()
    count, width = tok.shape
    half = count // 2
    slots = 2 * cap
    rows = 2 * slots
    meet(up, down, right)

    own = (tok, cot, info)
    ring = (tok_ring, cot_ring, info_ring)

    def slot(way, d):
        return FAR if d > HOPS else way * HOPS + d - 1

    def hop(q, way, d):
        src = own[q] if d == 1 else ring[q].at[slot(way, d - 1)]
        dst = ring[q].at[slot(way, d)]
        if d > HOPS and q < 2:
            src, dst = src.at[pl.ds(way * half, half)], dst.at[pl.ds(way * half, half)]
        sem = way * (HOPS + 1) + d - 1
        return copy_to(
            src, dst, ring_send.at[q, sem], ring_recv.at[q, sem], down if way else up
        )

    hops = {
        (q, way, d): hop(q, way, d)
        for q in range(3)
        for way in range(2)
        for d in range(1, HOPS + 2)
        if not (q == 2 and way == 1 and d > HOPS)
    }
    for q in (2, 0, 1):
        for way in range(2):
            hops[q, way, 1].start()

    lane = lax.broadcasted_iota(jnp.int32, (count, count), 1)
    before = lax.broadcasted_iota(jnp.int32, (count, count), 0)
    earlier = (before < lane).astype(BF16)
    place_row = lax.broadcasted_iota(jnp.int32, (rows, count), 0).astype(F32)
    caps = [(cap + cap * plan[z * COLS + (x + d) % COLS]).astype(F32) for d in range(COLS)]

    def choose(block, side):
        ids, gates = block[0:8, :], block[8:16, :]
        picks, weights = [], []
        for d in range(COLS):
            expert = (z * COLS + (x + d) % COLS).astype(F32)
            same = ids == expert
            picks.append(jnp.sum(jnp.where(same, 1.0, 0.0), axis=0, keepdims=True))
            weights.append(jnp.sum(jnp.where(same, gates, 0.0), axis=0, keepdims=True))
        picked = jnp.concatenate(picks + [jnp.zeros((8 - COLS, count), F32)], axis=0)
        rank = jnp.dot(picked.astype(BF16), earlier, preferred_element_type=F32)
        chosen = []
        for d in range(COLS):
            kept = (picks[d] > 0.5) & (rank[d : d + 1] < caps[d])
            spot = jnp.where(kept, rank[d : d + 1] + float(side * slots), -1.0)
            chosen.append(
                jnp.where(place_row == spot, jnp.broadcast_to(weights[d], (rows, count)), 0.0)
            )
        return jnp.concatenate(chosen, axis=0)

    row_copies = []
    own_copies = []

    def select(p, a, b):
        spread[p, 0] = choose(a[2], 0)
        spread[p, 1] = choose(b[2], 1)
        scale = jnp.sum(spread[p, 0] + spread[p, 1], axis=1, keepdims=True)
        one_a = jnp.where(spread[p, 0] > 0.0, 1.0, 0.0).astype(BF16)
        one_b = jnp.where(spread[p, 1] > 0.0, 1.0, 0.0).astype(BF16)
        step = 512
        for q, (sel, out) in enumerate(((tok_sel, tok_rows), (cot_sel, cot_rows))):

            @pl.loop(0, width // step)
            def _(i):
                cols = pl.ds(pl.multiple_of(i * step, step), step)
                got = jnp.dot(one_a, a[q][:, cols], preferred_element_type=F32)
                got += jnp.dot(one_b, b[q][:, cols], preferred_element_type=F32)
                if q == 1:
                    got = got * scale
                for d in range(COLS):
                    sel[p, d, :, cols] = got[d * rows : (d + 1) * rows].astype(BF16)

            for d in range(1, COLS):
                copy = copy_to(
                    sel.at[p, d], out.at[d, p], row_send.at[q, p, d - 1],
                    row_recv.at[q, p, d - 1], right[d],
                )
                copy.start()
                row_copies.append(copy)
            mine = pltpu.make_async_copy(sel.at[p, 0], out.at[0, p], own_sem.at[q, p])
            mine.start()
            own_copies.append(mine)

    def block(way, d):
        return tuple(ring[q].at[slot(way, d)] for q in range(3))

    for d in range(1, HOPS + 1):
        for q in (2, 0, 1):
            for way in range(2):
                if (q, way, d) in hops:
                    hops[q, way, d].wait_recv()
                if (q, way, d + 1) in hops:
                    hops[q, way, d + 1].start()
        select(d, block(0, d), block(1, d))
    for q in (2, 0, 1):
        for way in range(2):
            if (q, way, HOPS + 1) in hops:
                hops[q, way, HOPS + 1].wait_recv()
    select(0, own, block(0, HOPS + 1))

    for copy in hops.values():
        copy.wait_send()
    for copy in row_copies:
        copy.wait()
    for copy in own_copies:
        copy.wait()


def dispatch(cap, plan, tok, cot, info):
    count, width = tok.shape
    rows = 4 * cap
    shape = jax.ShapeDtypeStruct((COLS, PAIRS, rows, width), BF16)
    vmem = pl.BlockSpec(memory_space=pltpu.VMEM)
    hbm = pl.BlockSpec(memory_space=pl.ANY)
    return pl.pallas_call(
        functools.partial(dispatch_kernel, cap),
        name="dispatch",
        out_shape=(
            shape,
            shape,
            jax.ShapeDtypeStruct((PAIRS, 2, COLS * rows, count), F32),
        ),
        in_specs=[pl.BlockSpec(memory_space=pltpu.SMEM), vmem, vmem, vmem],
        out_specs=(hbm, hbm, vmem),
        scratch_shapes=[
            pltpu.VMEM((FAR + 1, count, width), BF16),
            pltpu.VMEM((FAR + 1, count, width), BF16),
            pltpu.VMEM((FAR + 1,) + info.shape, F32),
            pltpu.VMEM((PAIRS, COLS, rows, width), BF16),
            pltpu.VMEM((PAIRS, COLS, rows, width), BF16),
            pltpu.SemaphoreType.DMA((3, 2 * (HOPS + 1))),
            pltpu.SemaphoreType.DMA((3, 2 * (HOPS + 1))),
            pltpu.SemaphoreType.DMA((2, PAIRS, COLS - 1)),
            pltpu.SemaphoreType.DMA((2, PAIRS, COLS - 1)),
            pltpu.SemaphoreType.DMA((2, PAIRS)),
        ],
        compiler_params=pltpu.CompilerParams(
            collective_id=0, has_side_effects=True, vmem_limit_bytes=48 * 2**20
        ),
    )(plan, tok, cot, info)


def gather_kernel(
    out_rows, grad_rows, spread, out, grad,
    out_got, grad_got, mix, out_part, grad_part, out_in, grad_in,
    ring_send, ring_recv, row_send, row_recv, own_sem,
):
    z, x, up, down, right, left = place()
    count = spread.shape[3]
    half = count // 2
    meet(up, down, right)

    got = (out_got, grad_got)
    part = (out_part, grad_part)
    into = (out_in, grad_in)
    final = (out, grad)

    row_copies, own_copies = {}, {}
    for p in (0, 3, 2, 1):
        for q, src in enumerate((out_rows, grad_rows)):
            for d in range(1, COLS):
                row_copies[q, p, d] = copy_to(
                    src.at[d, p], got[q].at[p, d], row_send.at[q, p, d - 1],
                    row_recv.at[q, p, d - 1], left[d],
                )
                row_copies[q, p, d].start()
            own_copies[q, p] = pltpu.make_async_copy(
                src.at[0, p], got[q].at[p, 0], own_sem.at[q, p]
            )
            own_copies[q, p].start()

    for p in range(PAIRS):
        for side in range(2):
            turned = jnp.transpose(spread[p, side])
            high = turned.astype(BF16)
            mix[0, p, side] = high
            mix[1, p, side] = (turned - high.astype(F32)).astype(BF16)
            mix[2, p, side] = jnp.where(turned > 0.0, 1.0, 0.0).astype(BF16)

    step = 512

    def columns(q):
        width = got[q].shape[3]
        whole = width // step
        return whole, width - whole * step

    def each(q, body):
        whole, rest = columns(q)

        @pl.loop(0, whole)
        def _(i):
            body(pl.ds(pl.multiple_of(i * step, step), step))

        if rest:
            body(pl.ds(whole * step, rest))

    def combine(q, p, side, cols):
        slots = jnp.concatenate(
            [got[q][p, d, :, cols].astype(F32) for d in range(COLS)], axis=0
        ).astype(BF16)
        if q == 1:
            return jnp.dot(mix[2, p, side], slots, preferred_element_type=F32)
        total = jnp.dot(mix[0, p, side], slots, preferred_element_type=F32)
        return total + jnp.dot(mix[1, p, side], slots, preferred_element_type=F32)

    def hop(q, way, d):
        src, dst = part[q].at[way, d - 1], into[q].at[way, d - 1]
        if d > HOPS:
            src, dst = src.at[pl.ds(way * half, half)], dst.at[pl.ds(way * half, half)]
        sem = way * (HOPS + 1) + d - 1
        return copy_to(
            src, dst, ring_send.at[q, sem], ring_recv.at[q, sem], down if way else up
        )

    hops = {
        (q, way, d): hop(q, way, d)
        for q in range(2)
        for way in range(2)
        for d in range(1, HOPS + 2)
    }

    def arrive(q, p):
        for d in range(1, COLS):
            row_copies[q, p, d].wait_recv()
        own_copies[q, p].wait()

    for q in range(2):
        arrive(q, 0)

        def far(cols, q=q):
            total = combine(q, 0, 1, cols).astype(BF16)
            part[q][0, HOPS, 0:half, cols] = total[:half]
            part[q][1, HOPS, half:, cols] = total[half:]

        each(q, far)
        for way in range(2):
            hops[q, way, HOPS + 1].start()

    for d in range(HOPS, 0, -1):
        for q in range(2):
            arrive(q, d)
            for way in range(2):
                hops[q, way, d + 1].wait_recv()

                def near(cols, q=q, way=way, d=d):
                    total = combine(q, d, 1 - way, cols)
                    if d == HOPS:
                        mine = slice(half, None) if way else slice(0, half)
                        rest = slice(0, half) if way else slice(half, None)
                        there = into[q][way, d, mine, cols].astype(F32)
                        part[q][way, d - 1, mine, cols] = (total[mine] + there).astype(BF16)
                        part[q][way, d - 1, rest, cols] = total[rest].astype(BF16)
                    else:
                        there = into[q][way, d, :, cols].astype(F32)
                        part[q][way, d - 1, :, cols] = (total + there).astype(BF16)

                each(q, near)
                hops[q, way, d].start()

    for q in range(2):
        for way in range(2):
            hops[q, way, 1].wait_recv()

        def last(cols, q=q):
            total = combine(q, 0, 0, cols)
            total = total + into[q][0, 0, :, cols].astype(F32)
            total = total + into[q][1, 0, :, cols].astype(F32)
            final[q][:, cols] = total.astype(BF16)

        each(q, last)

    for copy in hops.values():
        copy.wait_send()
    for copy in row_copies.values():
        copy.wait_send()


def gather(out_rows, grad_rows, spread):
    rows, width = out_rows.shape[2:]
    wide = grad_rows.shape[3]
    count = spread.shape[3]
    vmem = pl.BlockSpec(memory_space=pltpu.VMEM)
    hbm = pl.BlockSpec(memory_space=pl.ANY)
    return pl.pallas_call(
        gather_kernel,
        name="gather",
        out_shape=(
            jax.ShapeDtypeStruct((count, width), BF16),
            jax.ShapeDtypeStruct((count, wide), BF16),
        ),
        in_specs=[hbm, hbm, vmem],
        out_specs=(vmem, vmem),
        scratch_shapes=[
            pltpu.VMEM((PAIRS, COLS, rows, width), BF16),
            pltpu.VMEM((PAIRS, COLS, rows, wide), BF16),
            pltpu.VMEM((3, PAIRS, 2, count, COLS * rows), BF16),
            pltpu.VMEM((2, HOPS + 1, count, width), BF16),
            pltpu.VMEM((2, HOPS + 1, count, wide), BF16),
            pltpu.VMEM((2, HOPS + 1, count, width), BF16),
            pltpu.VMEM((2, HOPS + 1, count, wide), BF16),
            pltpu.SemaphoreType.DMA((2, 2 * (HOPS + 1))),
            pltpu.SemaphoreType.DMA((2, 2 * (HOPS + 1))),
            pltpu.SemaphoreType.DMA((2, PAIRS, COLS - 1)),
            pltpu.SemaphoreType.DMA((2, PAIRS, COLS - 1)),
            pltpu.SemaphoreType.DMA((2, PAIRS)),
        ],
        compiler_params=pltpu.CompilerParams(
            collective_id=1, has_side_effects=True, vmem_limit_bytes=48 * 2**20
        ),
    )(out_rows, grad_rows, spread)


def expert_pass(rows, cots, weights, here):
    gate_part = jnp.dot(rows, weights[0], preferred_element_type=F32)
    up_part = jnp.dot(rows, weights[1], preferred_element_type=F32)
    sigma = jax.nn.sigmoid(gate_part)
    active = gate_part * sigma
    hidden = (active * up_part).astype(BF16)
    contract_last = (((1,), (1,)), ((), ()))
    out = lax.dot_general(hidden, weights[2], contract_last, preferred_element_type=F32)
    hgrad = jnp.dot(cots, weights[2], preferred_element_type=F32)
    d_gate = (hgrad * up_part * sigma * (1.0 + gate_part * (1.0 - sigma))).astype(BF16)
    d_up = (hgrad * active).astype(BF16)
    row_grad = lax.dot_general(d_gate, weights[0], contract_last, preferred_element_type=F32)
    row_grad += lax.dot_general(d_up, weights[1], contract_last, preferred_element_type=F32)
    inner = jnp.sum(hidden.astype(F32) * hgrad, axis=1, keepdims=True)
    lanes = lax.broadcasted_iota(jnp.int32, (rows.shape[0], LANES), 1)
    inner = jnp.where(lanes == here, inner, 0.0)
    grad = jnp.concatenate([row_grad.astype(BF16), inner.astype(BF16)], axis=1)
    contract_rows = (((0,), (0,)), ((), ()))
    upper = lax.dot_general(
        rows, jnp.concatenate([d_gate, d_up], axis=1), contract_rows, preferred_element_type=F32
    )
    lower = lax.dot_general(cots, hidden, contract_rows, preferred_element_type=F32)
    return out.astype(BF16), grad, jnp.concatenate([upper, lower], axis=1).astype(BF16)


def per_device(tokens, expert_ids, gate_vals, replica_plan, expert_weights, cotangent):
    count, width = tokens.shape
    topk = expert_ids.shape[1]
    experts = replica_plan.shape[0]
    hidden_units = expert_weights.shape[3]
    cap = count * topk * 5 // (16 * experts)
    here = lax.axis_index("expert")
    info = jnp.concatenate([expert_ids.astype(F32), gate_vals], axis=1).T
    tok_rows, cot_rows, spread = dispatch(cap, replica_plan, tokens, cotangent, info)
    shape = tok_rows.shape
    out, grad, partial = expert_pass(
        tok_rows.reshape(-1, width), cot_rows.reshape(-1, width), expert_weights[0], here
    )
    per_dev = width // lax.axis_size("dp")
    shard = lax.psum_scatter(partial, "dp", scatter_dimension=0, tiled=True)
    output, wide = gather(
        out.reshape(shape), grad.reshape(shape[:3] + (width + LANES,)), spread
    )
    input_grad = wide[:, :width]
    inner = wide[:, width : width + experts].astype(F32)
    labels = jnp.arange(experts, dtype=jnp.int32)
    same = expert_ids[:, :, None] == labels
    gate_grads = jnp.sum(jnp.where(same, inner[:, None, :], 0.0), axis=2) / gate_vals
    weight_grads = shard.reshape(per_dev, 3, hidden_units).transpose(1, 0, 2)[None]
    return (output, gate_grads, input_grad, weight_grads)


def solution(mesh):
    in_specs = (
        P(("dp", "expert"), None),
        P(("dp", "expert"), None),
        P(("dp", "expert"), None),
        P(),
        P("expert", None, None, None),
        P(("dp", "expert"), None),
    )
    out_specs = (
        P(("dp", "expert"), None),
        P(("dp", "expert"), None),
        P(("dp", "expert"), None),
        P("expert", None, "dp", None),
    )
    return jax.shard_map(
        per_device, mesh=mesh, in_specs=in_specs, out_specs=out_specs, check_vma=False
    )
```
